32 devices in a mesh: row: 4 (over y, x), col: 8 (over z, core).
Axes of the slice: x: 2, y: 2, z: 4, core: 2. Of those that a mesh axis runs over, the one named last changes fastest.
Arguments:
- queries: bfloat16 [8, 512, 1024], P('col', 'row'), may hold values from -120 to 120
- keys: bfloat16 [8, 512, 128], P('col', 'row'), may hold values from -8 to 8
- values: bfloat16 [8, 512, 128], P('col', 'row'), may hold values from -6 to 6
- outputs: bfloat16 [8, 512, 1024], P('col', 'row'), may hold values from -6 to 6
- out_grad: bfloat16 [8, 512, 1024], P('col', 'row'), may hold values from -192 to 192
- positions: int32 [8, 512], P('col'), may hold values from 0 to 511, each once within a row
- tile_flags: int32 [8, 4, 4], P('col', 'row'), may hold values 0 or 1
Outputs:
- query_grad: bfloat16 [8, 512, 1024], P('col', 'row')
- key_grad: bfloat16 [8, 512, 128], P('col', 'row')
- value_grad: bfloat16 [8, 512, 128], P('col', 'row')
The draws below stay inside these ranges and needn't reach their ends.
All inputs are finite; a program needn't handle non-finite values. No bound on the sum of `tile_flags` on one device may be relied on, other than what follows from the above.
Results may differ from the reference program's by a relative error of at most 0.0065.
Values may be sent and summed in bfloat16 or wider, within the bound.
No kernel may reach another device: no remote copies, remote signals or barrier semaphores. Data moves between devices by JAX's collectives and lax.ppermute only.
A program may use at most 64 MiB of HBM per device.

```python
import math
import jax
import jax.numpy as jnp
from jax import lax

H = 8
HD = 128
TOK_DEV = 128
LENGTH = 512
SEQS = 8
N_ROW = 4


def shared_draw(key):
    base_key = jax.random.fold_in(key, 7)
    first_key, second_key = jax.random.split(base_key, 2)
    total = SEQS * LENGTH
    key_rows = jnp.clip(jax.random.normal(first_key, (total, HD), jnp.float32), -6.0, 6.0)
    query_rows = jnp.clip(jax.random.normal(second_key, (total, H, HD), jnp.float32), -6.0, 6.0)
    return (query_rows.reshape(SEQS, LENGTH, H * HD), key_rows.reshape(SEQS, LENGTH, HD))


def draw_queries(key, part):
    return shared_draw(key)[0].astype(jnp.bfloat16)


def draw_keys(key, part):
    return shared_draw(key)[1].astype(jnp.bfloat16)


def set_ends(result, own_key, least, largest):
    dims = result.shape
    place = [jax.random.randint(jax.random.fold_in(own_key, axis), (), 0, dims[axis]) for axis in range(len(dims))]
    result = result.at[tuple(place)].set(least)
    longest = dims.index(max(dims))
    place[longest] = (place[longest] + 1) % dims[longest]
    return result.at[tuple(place)].set(largest)


def levels(stream_key, dims, cuts, least, largest):
    def one(dim, blocks):
        draws = jax.random.uniform(jax.random.fold_in(jax.random.fold_in(stream_key, 6), dim), (blocks,), jnp.float32, least / len(cuts), largest / len(cuts))
        return jnp.repeat(jnp.exp(draws), dims[dim] // blocks).reshape((-1,) + (1,) * (len(dims) - dim - 1))

    level = one(*cuts[0])
    for cut in cuts[1:]:
        level = level * one(*cut)
    return level


def normal_values(own_key, extent, scale, bound, cuts=(), kind=jnp.bfloat16):
    drawn = scale * jax.random.normal(own_key, extent, jnp.float32)
    if cuts:
        drawn = drawn * levels(own_key, extent, cuts, -0.22, 0.18)
    return jnp.clip(drawn, -bound, bound).astype(kind)


def setup_inputs(seed: int = 0) -> dict:
    streams_of = jax.random.split(jax.random.key(seed), 8)
    queries = draw_queries(jax.random.fold_in(streams_of[7], 71), 0)
    keys = draw_keys(jax.random.fold_in(streams_of[7], 71), 0)
    values = normal_values(streams_of[2], (SEQS, LENGTH, HD), 1.0, 6.0, ((0, 8), (1, 4)))
    outputs = normal_values(streams_of[3], (SEQS, LENGTH, H * HD), 1.0, 6.0, ((0, 8), (1, 4)))
    out_grad = normal_values(streams_of[4], (SEQS, LENGTH, H * HD), 32.0, 192.0, ((0, 8), (1, 4)))
    positions = jax.vmap(lambda own: jax.random.permutation(own, LENGTH))(jax.random.split(streams_of[5], SEQS)).reshape((SEQS, LENGTH)).astype(jnp.int32)
    tile_flags = set_ends((jax.random.randint(streams_of[6], (SEQS, N_ROW, N_ROW), 0, 2) < 1).astype(jnp.int32), jax.random.fold_in(streams_of[6], 1), 0, 1)
    return dict(queries=queries, keys=keys, values=values, outputs=outputs, out_grad=out_grad, positions=positions, tile_flags=tile_flags)


def one_trace(trace_in):
    query_seq, key_seq, value_seq, output_seq, grad_seq, pos_seq, flag_seq = trace_in
    score_scale = 1.0 / math.sqrt(HD)
    key_rows = key_seq.astype(jnp.float32)
    value_rows = value_seq.astype(jnp.float32)
    key_index = jnp.arange(LENGTH, dtype=jnp.int32)
    key_group = key_index // TOK_DEV

    def per_block(totals, block_in):
        key_total, value_total = totals
        query_block, grad_block, output_block, block_at = block_in
        query_heads = query_block.reshape(TOK_DEV, H, HD).astype(jnp.float32)
        grad_heads = grad_block.reshape(TOK_DEV, H, HD).astype(jnp.float32)
        output_heads = output_block.reshape(TOK_DEV, H, HD).astype(jnp.float32)
        query_index = block_at * TOK_DEV + jnp.arange(TOK_DEV, dtype=jnp.int32)
        query_pos = lax.dynamic_slice_in_dim(pos_seq, (block_at * TOK_DEV).astype(jnp.int32), TOK_DEV)
        key_flags = flag_seq[block_at][key_group]
        allowed = (pos_seq[None, :] <= query_pos[:, None]) & ((key_flags[None, :] == 1) | (key_index[None, :] == query_index[:, None]))
        scores = jnp.einsum('qhd,kd->hqk', query_heads, key_rows) * score_scale
        masked = jnp.where(allowed[None], scores, -1e+30)
        row_max = lax.optimization_barrier(jnp.max(masked, axis=2, keepdims=True))
        row_sum = lax.optimization_barrier(jnp.sum(jnp.where(allowed[None], jnp.exp(masked - row_max), 0.0), axis=2, keepdims=True))
        log_total = row_max + jnp.log(row_sum)
        weights = jnp.where(allowed[None], jnp.exp(masked - log_total), 0.0)
        out_dot = lax.optimization_barrier(jnp.sum(grad_heads * output_heads, axis=2)).T
        grad_probs = jnp.einsum('qhd,kd->hqk', grad_heads, value_rows)
        grad_scores = (weights * (grad_probs - out_dot[:, :, None]) * score_scale).astype(jnp.bfloat16)
        weights_low = weights.astype(jnp.bfloat16)
        grad_query = jnp.einsum('hqk,kd->qhd', grad_scores.astype(jnp.float32), key_rows)
        grad_query = grad_query.reshape(TOK_DEV, H * HD).astype(jnp.bfloat16)
        key_total = key_total + jnp.einsum('hqk,qhd->kd', grad_scores.astype(jnp.float32), query_heads)
        value_total = value_total + jnp.einsum('hqk,qhd->kd', weights_low.astype(jnp.float32), grad_heads)
        return ((key_total, value_total), grad_query)
    zeros = jnp.zeros((LENGTH, HD), jnp.float32)
    block_ids = jnp.arange(N_ROW, dtype=jnp.int32)
    block_in = (query_seq.reshape(N_ROW, TOK_DEV, H * HD), grad_seq.reshape(N_ROW, TOK_DEV, H * HD), output_seq.reshape(N_ROW, TOK_DEV, H * HD), block_ids)
    (key_total, value_total), query_grad = lax.scan(per_block, (zeros, zeros), block_in)
    return (query_grad.reshape(LENGTH, H * HD), key_total.astype(jnp.bfloat16), value_total.astype(jnp.bfloat16))

def reference(queries, keys, values, outputs, out_grad, positions, tile_flags):
    return lax.map(one_trace, (queries, keys, values, outputs, out_grad, positions, tile_flags))
```

```python
import functools
import math

import jax
import jax.numpy as jnp
from jax import lax
from jax.experimental import pallas as pl
from jax.experimental.pallas import tpu as pltpu
from jax.sharding import PartitionSpec as P

HD = 128
SCALE = 1.0 / math.sqrt(HD)
EXP2_SCALE = SCALE * math.log2(math.e)
MASKED = -1e30
F32 = jnp.float32
BF16 = jnp.bfloat16
VMEM = pl.BlockSpec(memory_space=pltpu.VMEM)
HBM = pl.BlockSpec(memory_space=pltpu.HBM)
SMEM = pl.BlockSpec(memory_space=pltpu.SMEM)
GRANT = pltpu.CompilerParams(vmem_limit_bytes=16 << 20)


def peer_of(rank, step, n):
    if n & (n - 1) == 0:
        return rank ^ step
    return lax.rem(rank + step, n) if isinstance(rank, jax.Array) else (rank + step) % n


def dot_nt(a, b):
    return lax.dot_general(a, b, (((1,), (1,)), ((), ())), preferred_element_type=F32)


def dot_nn(a, b):
    return lax.dot_general(a, b, (((1,), (0,)), ((), ())), preferred_element_type=F32)


def pack_kernel(k_ref, v_ref, kv_ref, sems):
    copies = [
        pltpu.make_async_copy(k_ref.at[0], kv_ref.at[:, :HD], sems.at[0]),
        pltpu.make_async_copy(v_ref.at[0], kv_ref.at[:, HD:], sems.at[1]),
    ]
    for copy in copies:
        copy.start()
    for copy in copies:
        copy.wait()


def pre_kernel(
    n, heads, rank_ref, flag_ref, pos_ref, q_hbm, g_hbm, o_hbm, kv_ref,
    bias_ref, dot_ref, top_ref, sum_ref, exp_ref, diff_ref, q_ref, g_ref, o_ref, sems,
):
    tokens = q_ref.shape[1]
    copies = [
        pltpu.make_async_copy(src, dst, sems.at[i])
        for i, (src, dst) in enumerate([(q_hbm, q_ref), (g_hbm, g_ref), (o_hbm, o_ref)])
    ]
    for copy in copies:
        copy.start()
    rank = rank_ref[0]
    pos = pos_ref[...].astype(F32)
    here = pos_ref[pl.ds(rank, 1), :].astype(F32)
    for step in range(n):
        peer = peer_of(rank, step, n)
        key_pos = jnp.broadcast_to(pos_ref[pl.ds(peer, 1), :].astype(F32), (8, tokens)).T[:, :1]
        seen = jnp.where(flag_ref[0, 0, peer] == 1, here, -1.0)
        allowed = key_pos <= seen
        if step == 0:
            rows = lax.broadcasted_iota(jnp.int32, (tokens, tokens), 0)
            cols = lax.broadcasted_iota(jnp.int32, (tokens, tokens), 1)
            allowed = allowed | (rows == cols)
        bias_ref[step] = jnp.where(allowed, 0.0, MASKED).astype(F32)
    key = kv_ref[:, :HD]
    value = kv_ref[:, HD:]
    for copy in copies:
        copy.wait()
    for h in range(heads):
        at = pl.ds(h * HD, HD)
        g = g_ref[0, :, at]
        out_dot = jnp.sum((g.astype(F32) * o_ref[0, :, at].astype(F32)).T, axis=0, keepdims=True)
        dot_ref[h : h + 1, :] = out_dot
        t = dot_nt(key, q_ref[0, :, at]) * EXP2_SCALE + bias_ref[0]
        top = jnp.max(t, axis=0, keepdims=True)
        e = jnp.exp2(t - top)
        top_ref[h : h + 1, :] = top
        sum_ref[h : h + 1, :] = jnp.sum(e, axis=0, keepdims=True)
        exp_ref[:, at] = e
        diff_ref[:, at] = (dot_nt(value, g) - out_dot) * SCALE


def main_kernel(
    n, heads, q_ref, g_ref, bias_ref, dot_ref, top_ref, sum_ref, *refs,
):
    kv_refs, refs = refs[: n - 1], refs[n - 1 :]
    part_refs, (fac_ref, ds_ref, p_ref) = refs[: n - 1], refs[n - 1 :]
    tokens = q_ref.shape[1]
    key = jnp.concatenate([r[:, :HD] for r in kv_refs], axis=0)
    value = jnp.concatenate([r[:, HD:] for r in kv_refs], axis=0)
    bias = bias_ref[1:].reshape((n - 1) * tokens, tokens)
    for h in range(heads):
        at = pl.ds(h * HD, HD)
        own_top = top_ref[h : h + 1, :]
        t = dot_nt(key, q_ref[0, :, at]) * EXP2_SCALE + bias
        top = jnp.maximum(own_top, jnp.max(t, axis=0, keepdims=True))
        e = jnp.exp2(t - top)
        own = jnp.exp2(own_top - top)
        inv = 1.0 / (own * sum_ref[h : h + 1, :] + jnp.sum(e, axis=0, keepdims=True))
        fac_ref[h : h + 1, :] = own * inv
        p = e * inv
        p_ref[:, at] = p.astype(BF16)
        diff = dot_nt(value, g_ref[0, :, at]) - dot_ref[h : h + 1, :]
        ds_ref[:, at] = (p * (diff * SCALE)).astype(BF16)
    key_sum, value_sum = 0.0, 0.0
    for h in range(0, heads, 2):
        at = pl.ds(h * HD, 2 * HD)
        q2 = jnp.concatenate([q_ref[0, :, pl.ds(i * HD, HD)] for i in (h, h + 1)], axis=0)
        g2 = jnp.concatenate([g_ref[0, :, pl.ds(i * HD, HD)] for i in (h, h + 1)], axis=0)
        key_sum = key_sum + dot_nn(ds_ref[:, at], q2)
        value_sum = value_sum + dot_nn(p_ref[:, at], g2)
    for s, part in enumerate(part_refs):
        rows = slice(s * tokens, (s + 1) * tokens)
        part[:, :HD] = key_sum[rows].astype(BF16)
        part[:, HD:] = value_sum[rows].astype(BF16)


def query_kernel(n, heads, q_ref, g_ref, exp_ref, diff_ref, fac_ref, ds_ref, kv_ref, *refs):
    kv_refs, (dq_ref, own_ref) = refs[: n - 1], refs[n - 1 :]
    tokens = q_ref.shape[1]
    key_t = jnp.concatenate([kv_ref[:, :HD]] + [r[:, :HD] for r in kv_refs], axis=0).T
    key_sum, value_sum = 0.0, 0.0
    for h in range(heads):
        at = pl.ds(h * HD, HD)
        p = exp_ref[:, at] * fac_ref[h : h + 1, :]
        ds = (p * diff_ref[:, at]).astype(BF16)
        key_sum = key_sum + dot_nn(ds, q_ref[0, :, at])
        value_sum = value_sum + dot_nn(p.astype(BF16), g_ref[0, :, at])
        ds_all = jnp.concatenate([ds, ds_ref[:, at]], axis=0)
        dq_ref[0, :, at] = dot_nn(key_t, ds_all).T.astype(BF16)
    own_ref[:, :HD] = key_sum
    own_ref[:, HD:] = value_sum


def sum_kernel(own_ref, *refs):
    parts, (dk_ref, dv_ref) = refs[:-2], refs[-2:]
    total = own_ref[...]
    for part in parts:
        total = total + part[...].astype(F32)
    dk_ref[0] = total[:, :HD].astype(BF16)
    dv_ref[0] = total[:, HD:].astype(BF16)


def body(n, queries, keys, values, outputs, out_grad, positions, tile_flags):
    tokens, width = queries.shape[1:]
    heads = width // HD
    rank = lax.axis_index("row").astype(jnp.int32).reshape(1)
    pos = positions.reshape(n, tokens)
    sds = jax.ShapeDtypeStruct
    rows = (n - 1) * tokens

    def there(step):
        return [(i, peer_of(i, step, n)) for i in range(n)]

    def back(step):
        return [(j, i) for i, j in there(step)]

    keys, values, far_q, far_g, far_o = (
        pltpu.with_memory_space_constraint(x, pltpu.HBM) for x in (keys, values, queries, out_grad, outputs)
    )
    kv = pl.pallas_call(
        pack_kernel,
        out_shape=sds((tokens, 2 * HD), BF16),
        in_specs=[HBM] * 2,
        out_specs=VMEM,
        compiler_params=GRANT,
        scratch_shapes=[pltpu.SemaphoreType.DMA((2,))],
    )(keys, values)
    kv_far = [lax.ppermute(kv, "row", back(s)) for s in range(1, n)]
    bias, out_dot, top, total, e_own, diff, q_near, g_near = pl.pallas_call(
        functools.partial(pre_kernel, n, heads),
        out_shape=(
            sds((n, tokens, tokens), F32),
            sds((heads, tokens), F32),
            sds((heads, tokens), F32),
            sds((heads, tokens), F32),
            sds((tokens, width), F32),
            sds((tokens, width), F32),
            sds((1, tokens, width), BF16),
            sds((1, tokens, width), BF16),
        ),
        in_specs=[SMEM, SMEM, VMEM, HBM, HBM, HBM, VMEM],
        out_specs=(VMEM,) * 8,
        scratch_shapes=[pltpu.VMEM((1, tokens, width), BF16), pltpu.SemaphoreType.DMA((3,))],
        compiler_params=GRANT,
    )(rank, tile_flags, pos, far_q, far_g, far_o, kv)
    outs = pl.pallas_call(
        functools.partial(main_kernel, n, heads),
        out_shape=(sds((tokens, 2 * HD), BF16),) * (n - 1)
        + (sds((heads, tokens), F32), sds((rows, width), BF16)),
        in_specs=[VMEM] * (6 + n - 1),
        out_specs=(VMEM,) * (n + 1),
        compiler_params=GRANT,
        scratch_shapes=[pltpu.VMEM((rows, width), BF16)],
    )(q_near, g_near, bias, out_dot, top, total, *kv_far)
    parts, fac, ds = outs[: n - 1], outs[n - 1], outs[n]
    parts_in = [lax.ppermute(part, "row", there(s)) for s, part in list(zip(range(1, n), parts))[::-1]]
    query_grad, own = pl.pallas_call(
        functools.partial(query_kernel, n, heads),
        out_shape=(sds((1, tokens, width), BF16), sds((tokens, 2 * HD), F32)),
        in_specs=[VMEM] * (7 + n - 1),
        out_specs=(VMEM,) * 2,
        compiler_params=GRANT,
    )(q_near, g_near, e_own, diff, fac, ds, kv, *kv_far)
    key_grad, value_grad = pl.pallas_call(
        sum_kernel,
        out_shape=(sds((1, tokens, HD), BF16),) * 2,
        in_specs=[VMEM] * n,
        out_specs=(VMEM,) * 2,
        compiler_params=GRANT,
    )(own, *parts_in)
    return query_grad, key_grad, value_grad


def solution(mesh):
    whole = P("col", "row", None)
    return jax.shard_map(
        functools.partial(body, mesh.shape["row"]),
        mesh=mesh,
        in_specs=(whole,) * 5 + (P("col", None), whole),
        out_specs=(whole,) * 3,
        check_vma=False,
    )
```
